128 devices in a mesh: ctx: 32 (over x, y, core), tp: 4 (over z).
Axes of the slice: x: 4, y: 4, z: 4, core: 2. Of those that a mesh axis runs over, the one named last changes fastest.
Arguments:
- attention: bfloat16 [16384, 2048], P('ctx', 'tp'), may hold values from -6 to 6
- residual: bfloat16 [16384, 2048], P(('ctx', 'tp')), may hold values from -6 to 6
- w_out: bfloat16 [2048, 2048], P('tp'), may hold values from -0.125 to 0.125
- w_qkv: bfloat16 [3072, 2048], P('tp'), may hold values from -0.125 to 0.125
- norm_moe: float32 [2048], replicated, may hold values from 0.25 to 1.75
- norm_attn: float32 [2048], replicated, may hold values from 0.25 to 1.75
- expert_ids: int32 [16384, 4], P(('ctx', 'tp')), may hold values from 0 to 63, all different within a row; in each aligned block of 128 rows (0 to 127, 128 to 255, ...) at most 12 rows name the same one
- expert_gates: float32 [16384, 4], P(('ctx', 'tp')), may hold values from 0.02 to 0.3
- w_gate: bfloat16 [128, 2048, 384], P(('ctx', 'tp')), may hold values from -0.125 to 0.125
- w_up: bfloat16 [128, 2048, 384], P(('ctx', 'tp')), may hold values from -0.125 to 0.125
- w_down: bfloat16 [128, 384, 2048], P(('ctx', 'tp')), may hold values from -0.21875 to 0.21875
- d_projected: bfloat16 [16384, 3072], P('ctx', 'tp'), may hold values from -6 to 6
- d_stream: bfloat16 [16384, 2048], P(('ctx', 'tp')), may hold values from -6 to 6
Outputs:
- projected: bfloat16 [16384, 3072], P('ctx', 'tp')
- stream: bfloat16 [16384, 2048], P(('ctx', 'tp'))
- grad_attention: bfloat16 [16384, 2048], P('ctx', 'tp')
- grad_residual: bfloat16 [16384, 2048], P(('ctx', 'tp'))
- grad_w_out: bfloat16 [2048, 2048], P('tp', 'ctx')
- grad_w_gate: bfloat16 [128, 2048, 384], P(('ctx', 'tp'))
- grad_w_up: bfloat16 [128, 2048, 384], P(('ctx', 'tp'))
- grad_w_down: bfloat16 [128, 384, 2048], P(('ctx', 'tp'))
The draws below stay inside these ranges and needn't reach their ends.
Inputs may be any that keep to these rules, and one draw needn't show every extreme that they name: `expert_ids`: each row names 4 different experts. Among the rows of one device no expert is named more than 12 times, a bound that some block reaches there.
All inputs are finite; a program needn't handle non-finite values.
Results may differ from the reference program's by a relative error of at most 0.0075.
Values may be sent and summed in bfloat16 or wider, within the bound.
No kernel may reach another device: no remote copies, remote signals or barrier semaphores. Data moves between devices by JAX's collectives and lax.ppermute only.
A program may use at most 128 MiB of HBM per device.

```python
import math
import jax
import jax.numpy as jnp
import numpy as np
from jax import lax

D = 2048
FF = 768
TOPK = 4
QD = 2048
QKV = 3072
TOK_DEV = 512
TOKENS = 16384
EXPERTS = 64
HALVES = 128
CAP = 12
N_CTX = 32
N_TP = 4


def block_scale(key, shape, cuts, smallest, top_value):
    def one(dim, blocks):
        draws = jax.random.uniform(jax.random.fold_in(jax.random.fold_in(key, 6), dim), (blocks,), jnp.float32, smallest / len(cuts), top_value / len(cuts))
        return jnp.repeat(jnp.exp(draws), shape[dim] // blocks).reshape((-1,) + (1,) * (len(shape) - dim - 1))

    gain = one(*cuts[0])
    for cut in cuts[1:]:
        gain = gain * one(*cut)
    return gain


def assign_block(key, own, number, rows, number_of, top, most, lean):
    sequence = jax.random.permutation(key, number_of)
    crowded, ordinary = shares(number_of, rows * top, most, lean, True), shares(number_of, rows * top, most, lean, False)
    places = jnp.arange(number_of)

    def named(sizes, turn):
        used = int((sizes > 0).sum())
        fixed = max(1, used // 4)
        shifted = fixed + (places - fixed + turn * (used - fixed)) % max(1, number_of - fixed)
        return jnp.zeros((number_of,), jnp.int32).at[sequence[jnp.where(places < fixed, places, shifted)]].set(jnp.asarray(sizes, jnp.int32))

    sizes = jnp.where(number % 4 == 0, named(crowded, number // 4), named(ordinary, number - number // 4 - 1))
    mixed = jax.random.permutation(jax.random.fold_in(own, 3), number_of)
    donor, sink = mixed[0:number_of // 2 * 2:2], mixed[1:number_of // 2 * 2:2]
    margin = jnp.minimum(sizes[donor] - 1, most - sizes[sink]) // 2
    margin = jnp.where((donor == sequence[0]) | (sink == sequence[0]) | (sizes[sink] == 0), 0, jnp.maximum(margin, 0))
    shifted = jax.random.randint(jax.random.fold_in(own, 4), (number_of // 2,), 0, 1 << 20) % (margin + 1)
    sizes = sizes.at[donor].add(-shifted).at[sink].add(shifted)
    members = jnp.searchsorted(jnp.cumsum(sizes), jnp.arange(rows * top), side="right").astype(jnp.int32)
    listing = members.reshape(top, rows).T
    listing = listing[jax.random.permutation(jax.random.fold_in(own, 1), rows)]
    turn = jax.random.randint(jax.random.fold_in(own, 2), (rows, 1), 0, top)
    return jnp.take_along_axis(listing, (jnp.arange(top)[None, :] + turn) % top, axis=1)


def shares(amount, total, reach, slope, full):
    portions = [(1 << 20) // math.isqrt(grade ** slope) + 1 for grade in range(1, amount + 1)]
    largest = reach if full else min(reach, max(-(-total // amount), total * portions[0] // sum(portions)))
    least = 1 if total - largest >= amount - 1 else 0
    counts, spare = [largest] + [least] * (amount - 1), total - largest - least * (amount - 1)
    while spare > 0:
        free = [i for i in range(1, amount) if counts[i] < largest] or [i for i in range(1, amount) if counts[i] < reach]
        whole, budget = sum([portions[i] for i in free]), spare
        for i in free:
            more = min(reach - counts[i], max(1, budget * portions[i] // whole), spare)
            counts[i] = counts[i] + more
            spare = spare - more
    return np.array(counts)


def centred(key, shape, width, bound, split=(), kind=jnp.bfloat16):
    factor_of = block_scale(key, shape, split, -0.22, 0.18) if split else 1.0
    entries = jax.random.normal(key, shape, jnp.float32) * width * factor_of
    return jnp.minimum(jnp.maximum(entries, -bound), bound).astype(kind)


def setup_inputs(seed: int = 0) -> dict:
    splits = jax.random.split(jax.random.key(seed), 14)
    attention = centred(splits[0], (TOKENS, QD), 1.0, 6.0, ((0, 32), (1, 4)))
    residual = centred(splits[1], (TOKENS, D), 1.0, 6.0, ((0, 128),))
    w_out = centred(splits[2], (QD, D), QD ** -0.5, 0.125, ((0, 4),))
    w_qkv = centred(splits[3], (QKV, D), D ** -0.5, 0.125, ((0, 4),))
    norm_moe = jnp.clip(1.0 + 0.15 * jax.random.normal(splits[4], (D,), jnp.float32), 0.25, 1.75)
    norm_attn = jnp.clip(1.0 + 0.15 * jax.random.normal(splits[5], (D,), jnp.float32), 0.25, 1.75)
    expert_ids_keys = jax.random.split(jax.random.fold_in(splits[6], 1), TOKENS // (TOK_DEV // N_TP))
    expert_ids_turns = jax.random.permutation(jax.random.fold_in(splits[6], 3), TOKENS // (TOK_DEV // N_TP))
    expert_ids = jax.vmap(lambda own, number: assign_block(jax.random.fold_in(splits[6], 2), own, number, TOK_DEV // N_TP, EXPERTS, TOPK, CAP, 2))(expert_ids_keys, expert_ids_turns).reshape((TOKENS, TOPK))
    expert_gates = jnp.clip(0.02 + 0.28 * jax.random.uniform(splits[7], (TOKENS, TOPK), jnp.float32) ** block_scale(splits[7], (TOKENS, TOPK), ((0, 128),), -0.2, 0.2), 0.02, 0.3)
    w_gate = centred(splits[8], (HALVES, D, FF // 2), D ** -0.5, 0.125, ((0, 128),))
    w_up = centred(splits[9], (HALVES, D, FF // 2), D ** -0.5, 0.125, ((0, 128),))
    w_down = centred(splits[10], (HALVES, FF // 2, D), FF ** -0.5, 0.21875, ((0, 128),))
    d_projected = centred(splits[11], (TOKENS, QKV), 1.0, 6.0, ((0, 32), (1, 4)))
    d_stream = centred(splits[12], (TOKENS, D), 1.0, 6.0, ((0, 128),))
    return {"attention": attention, "residual": residual, "w_out": w_out, "w_qkv": w_qkv, "norm_moe": norm_moe, "norm_attn": norm_attn, "expert_ids": expert_ids, "expert_gates": expert_gates, "w_gate": w_gate, "w_up": w_up, "w_down": w_down, "d_projected": d_projected, "d_stream": d_stream}


EPSILON = 1e-06

def rms_inverse(hidden):
    return lax.rsqrt(lax.optimization_barrier(jnp.mean(hidden * hidden, axis=-1, keepdims=True)) + EPSILON)

def rms_grad(hidden, gain_vec, inv_rms, grad_out):
    normed = hidden * inv_rms
    grad_normed = grad_out * gain_vec
    return inv_rms * (grad_normed - normed * lax.optimization_barrier(jnp.mean(grad_normed * normed, axis=-1, keepdims=True)))

def expert_inner(slot_rows, gate_mat, up_mat):
    pre_gate = jnp.dot(slot_rows, gate_mat, preferred_element_type=jnp.float32)
    pre_up = jnp.dot(slot_rows, up_mat, preferred_element_type=jnp.float32)
    active = (jax.nn.silu(pre_gate) * pre_up).astype(jnp.bfloat16)
    return (pre_gate, pre_up, active)

def half_backward(slot_rows, slot_grads, pre_gate, pre_up, active, gate_mat, up_mat, down_mat):
    sigmoid_gate = jax.nn.sigmoid(pre_gate)
    silu_gate = pre_gate * sigmoid_gate
    grad_active = jnp.einsum('sd,fd->sf', slot_grads, down_mat, preferred_element_type=jnp.float32)
    grad_gate = (grad_active * pre_up * sigmoid_gate * (1.0 + pre_gate * (1.0 - sigmoid_gate))).astype(jnp.bfloat16)
    grad_up = (grad_active * silu_gate).astype(jnp.bfloat16)
    input_part = jnp.einsum('sf,df->sd', grad_gate, gate_mat, preferred_element_type=jnp.float32)
    input_part = (input_part + jnp.einsum('sf,df->sd', grad_up, up_mat, preferred_element_type=jnp.float32)).astype(jnp.bfloat16)
    gate_term = jnp.einsum('sd,sf->df', slot_rows, grad_gate, preferred_element_type=jnp.float32)
    up_term = jnp.einsum('sd,sf->df', slot_rows, grad_up, preferred_element_type=jnp.float32)
    down_term = jnp.einsum('sf,sd->fd', active, slot_grads, preferred_element_type=jnp.float32)
    return (input_part, gate_term, up_term, down_term)

def slot_tables(expert_ids, expert_gates):
    devices = N_CTX * N_TP
    per_device = TOKENS // devices
    blocks = expert_ids.reshape(devices, per_device * TOPK)
    expert_range = jnp.arange(EXPERTS, dtype=jnp.int32)
    onehot = (blocks[:, :, None] == expert_range[None, None, :]).astype(jnp.int32)
    position = lax.optimization_barrier(jnp.sum((jnp.cumsum(onehot, axis=1) - onehot) * onehot, axis=2))
    device_of = jnp.arange(devices, dtype=jnp.int32)[:, None]
    column = (device_of * CAP + position).reshape(-1).astype(jnp.int32)
    token_index = (jnp.arange(TOKENS * TOPK, dtype=jnp.int32) // TOPK).astype(jnp.int32)
    flat_ids = expert_ids.reshape(-1)
    token_of = jnp.full((EXPERTS, devices * CAP), TOKENS, jnp.int32).at[flat_ids, column].set(token_index)
    gate_of = jnp.zeros((EXPERTS, devices * CAP), jnp.float32).at[flat_ids, column].set(expert_gates.reshape(-1))
    return (token_of, gate_of)

def reference(attention, residual, w_out, w_qkv, norm_moe, norm_attn, expert_ids, expert_gates, w_gate, w_up, w_down, d_projected, d_stream):
    half_width = FF // 2
    hidden = residual.astype(jnp.float32) + jnp.dot(attention, w_out, preferred_element_type=jnp.float32)
    inv_one = rms_inverse(hidden)
    moe_input = (hidden * inv_one * norm_moe).astype(jnp.bfloat16)
    token_of, gate_of = slot_tables(expert_ids, expert_gates)
    input_pad = jnp.concatenate([moe_input, jnp.zeros((1, D), jnp.bfloat16)], axis=0)
    gate_pairs = w_gate.reshape(EXPERTS, 2, D, half_width)
    up_pairs = w_up.reshape(EXPERTS, 2, D, half_width)
    down_pairs = w_down.reshape(EXPERTS, 2, half_width, D)

    def forward_expert(running, inputs):
        gate_pair, up_pair, down_pair, tokens_here, gates_here = inputs
        slot_rows = input_pad[tokens_here]
        first = jnp.dot(expert_inner(slot_rows, gate_pair[0], up_pair[0])[2], down_pair[0], preferred_element_type=jnp.float32).astype(jnp.bfloat16)
        second = jnp.dot(expert_inner(slot_rows, gate_pair[1], up_pair[1])[2], down_pair[1], preferred_element_type=jnp.float32).astype(jnp.bfloat16)
        output = (first.astype(jnp.float32) + second.astype(jnp.float32)).astype(jnp.bfloat16)
        return (running.at[tokens_here].add(gates_here[:, None] * output.astype(jnp.float32)), None)
    moe_sum = lax.scan(forward_expert, jnp.zeros((TOKENS + 1, D), jnp.float32), (gate_pairs, up_pairs, down_pairs, token_of, gate_of))[0]
    stream_sum = hidden + moe_sum[:TOKENS]
    stream = stream_sum.astype(jnp.bfloat16)
    inv_two = rms_inverse(stream_sum)
    attn_input = (stream_sum * inv_two * norm_attn).astype(jnp.bfloat16)
    projected = jnp.dot(attn_input, w_qkv.T, preferred_element_type=jnp.float32).astype(jnp.bfloat16)
    grad_attn_in = jnp.dot(d_projected, w_qkv, preferred_element_type=jnp.float32)
    grad_stream = d_stream.astype(jnp.float32) + rms_grad(stream_sum, norm_attn, inv_two, grad_attn_in)
    grad_pad = jnp.concatenate([grad_stream, jnp.zeros((1, D), jnp.float32)], axis=0)

    def backward_expert(running, inputs):
        gate_pair, up_pair, down_pair, tokens_here, gates_here = inputs
        slot_rows = input_pad[tokens_here]
        slot_grads = (gates_here[:, None] * grad_pad[tokens_here]).astype(jnp.bfloat16)
        parts = []
        gate_terms = []
        up_terms = []
        down_terms = []
        for half in range(2):
            pre_gate, pre_up, active = expert_inner(slot_rows, gate_pair[half], up_pair[half])
            input_part, gate_term, up_term, down_term = half_backward(slot_rows, slot_grads, pre_gate, pre_up, active, gate_pair[half], up_pair[half], down_pair[half])
            parts.append(input_part.astype(jnp.float32))
            gate_terms.append(gate_term.astype(jnp.bfloat16))
            up_terms.append(up_term.astype(jnp.bfloat16))
            down_terms.append(down_term.astype(jnp.bfloat16))
        grad_input = (parts[0] + parts[1]).astype(jnp.bfloat16)
        stacked = (jnp.stack(gate_terms), jnp.stack(up_terms), jnp.stack(down_terms))
        return (running.at[tokens_here].add(grad_input.astype(jnp.float32)), stacked)
    grad_moe_pad, weight_grads = lax.scan(backward_expert, jnp.zeros((TOKENS + 1, D), jnp.float32), (gate_pairs, up_pairs, down_pairs, token_of, gate_of))
    grad_hidden = grad_stream + rms_grad(hidden, norm_moe, inv_one, grad_moe_pad[:TOKENS])
    grad_residual = grad_hidden.astype(jnp.bfloat16)
    grad_attention = jnp.dot(grad_residual, w_out.T, preferred_element_type=jnp.float32).astype(jnp.bfloat16)
    grad_w_out = jnp.dot(attention.T, grad_residual, preferred_element_type=jnp.float32).astype(jnp.bfloat16)
    grad_w_gate = weight_grads[0].reshape(HALVES, D, half_width)
    grad_w_up = weight_grads[1].reshape(HALVES, D, half_width)
    grad_w_down = weight_grads[2].reshape(HALVES, half_width, D)
    return (projected, stream, grad_attention, grad_residual, grad_w_out, grad_w_gate, grad_w_up, grad_w_down)
```

```python
import jax
import jax.numpy as jnp
from jax import lax
from jax.sharding import PartitionSpec as P

EPSILON = 1e-06
BF = jnp.bfloat16
F32 = jnp.float32
CAP = 12
TP = 4

UP = [(i, (i + 1) % TP) for i in range(TP)]
DOWN = [(i, (i - 1) % TP) for i in range(TP)]
MIRROR = [(i, TP - 1 - i) for i in range(TP)]
TWIN = [(i, i ^ 1) for i in range(TP)]


def shift(block, route):
    return lax.ppermute(block, "tp", route)


def dotf(a, b, dims=((1,), (0,))):
    return lax.dot_general(a, b, (dims, ((), ())), preferred_element_type=F32)


def rms_inverse(hidden):
    return lax.rsqrt(jnp.mean(hidden * hidden, axis=-1, keepdims=True) + EPSILON)


def rms_grad(hidden, gain_vec, inv_rms, grad_out):
    normed = hidden * inv_rms
    grad_normed = grad_out * gain_vec
    return inv_rms * (grad_normed - normed * jnp.mean(grad_normed * normed, axis=-1, keepdims=True))


def block_of(rows, offset):
    z = lax.axis_index("tp")
    parts = rows.reshape(TP, rows.shape[0] // TP, rows.shape[1])
    return lax.dynamic_index_in_dim(parts, (z + offset) % TP, 0, keepdims=False)


def ring_reduce(source, weights):
    half = weights.shape[1] // 2
    far = dotf(block_of(source, 2), weights).astype(BF)
    from_below = shift(far[:, :half], UP)
    from_above = shift(far[:, half:], DOWN)
    above = dotf(block_of(source, 1), weights)
    below = dotf(block_of(source, 3), weights)
    to_above = jnp.concatenate([above[:, :half] + from_below.astype(F32), above[:, half:]], 1)
    to_below = jnp.concatenate([below[:, :half], below[:, half:] + from_above.astype(F32)], 1)
    got_up = shift(to_above.astype(BF), UP)
    got_down = shift(to_below.astype(BF), DOWN)
    own = dotf(block_of(source, 0), weights)
    return own + got_up.astype(F32) + got_down.astype(F32)


def ring_gather(rows):
    half = rows.shape[1] // 2
    below = shift(rows, UP)
    above = shift(rows, DOWN)
    far_left = shift(below[:, :half], UP)
    far_right = shift(above[:, half:], DOWN)
    return rows, above, jnp.concatenate([far_left, far_right], 1), below


def place(blocks):
    z = lax.axis_index("tp")
    out = jnp.zeros((TP,) + blocks[0].shape, blocks[0].dtype)
    for j, block in enumerate(blocks):
        out = lax.dynamic_update_index_in_dim(out, block, (z + j) % TP, 0)
    return out.reshape(TP * blocks[0].shape[0], blocks[0].shape[1])


def exchange(rows, ctx_count):
    width = rows.shape[1]
    blocks = rows.reshape(ctx_count, rows.shape[0] // ctx_count, width)
    moved = lax.all_to_all(blocks, "ctx", split_axis=0, concat_axis=0, tiled=True)
    return moved.reshape(rows.shape)


def local(
    attention,
    residual,
    w_out,
    w_qkv,
    norm_moe,
    norm_attn,
    expert_ids,
    expert_gates,
    w_gate,
    w_up,
    w_down,
    d_projected,
    d_stream,
):
    ctx_count = lax.axis_size("ctx")
    z = lax.axis_index("tp")
    tokens, width = residual.shape
    kind = z // 2

    gate_mine, up_mine, down_mine = w_gate[0], w_up[0], w_down[0]
    ff = gate_mine.shape[1]
    gate_twin = shift(gate_mine, TWIN)
    up_twin = shift(up_mine, TWIN)
    down_twin = shift(down_mine, TWIN)

    table = jnp.concatenate([expert_ids.astype(F32), expert_gates], 1).T
    table = jnp.concatenate([table, shift(table, MIRROR)], 1)
    top = expert_ids.shape[1]
    ids_t = table[:top].astype(jnp.int32)
    gates_t = table[top:]
    wanted = 2 * jnp.arange(ctx_count, dtype=jnp.int32) + kind
    same = ids_t[:, None, :] == wanted[None, :, None]
    member = jnp.any(same, axis=0)
    gate_of = jnp.sum(jnp.where(same, gates_t[:, None, :], 0.0), axis=0)
    token = jnp.arange(2 * tokens, dtype=jnp.int32)
    earlier = (token[:, None] < token[None, :]) & (
        token[:, None] // tokens == token[None, :] // tokens
    )
    position = dotf(member.astype(BF), earlier.astype(BF)).astype(jnp.int32)
    position = position + CAP * (token // tokens)[None, :]
    position = jnp.where(member, position, -1)
    row = jnp.arange(2 * CAP, dtype=jnp.int32)
    chosen = position[:, None, :] == row[None, :, None]
    slots = ctx_count * 2 * CAP
    select = chosen.astype(BF).reshape(slots, 2 * tokens)
    gated = jnp.where(chosen, gate_of[:, None, :], 0.0).reshape(slots, 2 * tokens)
    gate_slot = jnp.sum(gated, axis=1, keepdims=True)
    gated_hi = gated.astype(BF)
    gated_lo = (gated - gated_hi.astype(F32)).astype(BF)

    hidden = residual.astype(F32) + ring_reduce(attention, w_out)
    inv_one = rms_inverse(hidden)
    moe_input = (hidden * inv_one * norm_moe).astype(BF)
    inputs = jnp.concatenate([moe_input, shift(moe_input, MIRROR)], 0)
    arrived = exchange(dotf(select, inputs).astype(BF), ctx_count)

    w_all = jnp.concatenate([gate_mine, up_mine, gate_twin, up_twin], 1)
    down_all = jnp.concatenate([down_mine, down_twin], 0)
    pre = dotf(arrived, w_all)
    pre_gate = jnp.concatenate([pre[:, :ff], pre[:, 2 * ff : 3 * ff]], 1)
    pre_up = jnp.concatenate([pre[:, ff : 2 * ff], pre[:, 3 * ff :]], 1)
    active = (jax.nn.silu(pre_gate) * pre_up).astype(BF)
    produced = dotf(active, down_all).astype(BF)
    returned = exchange(produced, ctx_count)

    over = ((0,), (0,))
    moe_mirror = dotf(gated_hi[:, tokens:], returned, over) + dotf(
        gated_lo[:, tokens:], returned, over
    )
    moe_got = shift(moe_mirror.astype(BF), MIRROR)
    moe_own = dotf(gated_hi[:, :tokens], returned, over) + dotf(
        gated_lo[:, :tokens], returned, over
    )
    stream_sum = hidden + (moe_own + moe_got.astype(F32))
    stream = stream_sum.astype(BF)
    inv_two = rms_inverse(stream_sum)
    attn_input = (stream_sum * inv_two * norm_attn).astype(BF)

    grad_attn_in = ring_reduce(d_projected, w_qkv)
    grad_stream = d_stream.astype(F32) + rms_grad(stream_sum, norm_attn, inv_two, grad_attn_in)
    grad_bf = grad_stream.astype(BF)
    grad_pair = jnp.concatenate([grad_bf, shift(grad_bf, MIRROR)], 0)
    grad_slots = (dotf(select, grad_pair) * gate_slot).astype(BF)
    grads = exchange(grad_slots, ctx_count)

    sigmoid_gate = jax.nn.sigmoid(pre_gate)
    grad_active = dotf(grads, down_all, ((1,), (1,)))
    grad_gate = (
        grad_active * pre_up * sigmoid_gate * (1.0 + pre_gate * (1.0 - sigmoid_gate))
    ).astype(BF)
    grad_up = (grad_active * (pre_gate * sigmoid_gate)).astype(BF)
    grad_mine = jnp.concatenate([grad_gate[:, :ff], grad_up[:, :ff]], 1)
    grad_twin = jnp.concatenate([grad_gate[:, ff:], grad_up[:, ff:]], 1)
    grad_all = jnp.concatenate([grad_mine, grad_twin], 1)
    grad_input = dotf(grad_all, w_all, ((1,), (1,))).astype(BF)

    down_got = shift(dotf(active[:, ff:], grads, over).astype(BF), TWIN)
    pair_got = shift(dotf(arrived, grad_twin, over).astype(BF), TWIN)
    back = exchange(grad_input, ctx_count)

    moe_grad_mirror = dotf(select[:, tokens:], back, over)
    moe_grad_got = shift(moe_grad_mirror.astype(BF), MIRROR)
    grad_moe_in = dotf(select[:, :tokens], back, over) + moe_grad_got.astype(F32)
    grad_hidden = grad_stream + rms_grad(hidden, norm_moe, inv_one, grad_moe_in)
    grad_residual = grad_hidden.astype(BF)

    grad_blocks = ring_gather(grad_residual)
    grad_rows = jnp.concatenate(grad_blocks, 0)
    attn_rel = jnp.concatenate([block_of(attention, j) for j in range(TP)], 0)
    out_partial = dotf(grad_rows, attn_rel, over).astype(BF)
    out_moved = lax.all_to_all(
        out_partial.reshape(ctx_count, width // ctx_count, attention.shape[1]),
        "ctx",
        split_axis=0,
        concat_axis=0,
        tiled=True,
    )
    out_weight_grad = jnp.sum(out_moved.astype(F32), axis=0).T.astype(BF)
    grad_attention = place([dotf(g, w_out, ((1,), (1,))).astype(BF) for g in grad_blocks])
    projected = place(
        [dotf(a, w_qkv, ((1,), (1,))).astype(BF) for a in ring_gather(attn_input)]
    )

    down_grad = (dotf(active[:, :ff], grads, over) + down_got.astype(F32)).astype(BF)
    pair_grad = (dotf(arrived, grad_mine, over) + pair_got.astype(F32)).astype(BF)
    return (
        projected,
        stream,
        grad_attention,
        grad_residual,
        out_weight_grad,
        pair_grad[:, :ff][None],
        pair_grad[:, ff:][None],
        down_grad[None],
    )


def solution(mesh):
    token_rows = P(("ctx", "tp"), None)
    experts = P(("ctx", "tp"), None, None)
    in_specs = (
        P("ctx", "tp"),
        token_rows,
        P("tp", None),
        P("tp", None),
        P(),
        P(),
        token_rows,
        token_rows,
        experts,
        experts,
        experts,
        P("ctx", "tp"),
        token_rows,
    )
    out_specs = (
        P("ctx", "tp"),
        token_rows,
        P("ctx", "tp"),
        token_rows,
        P("tp", "ctx"),
        experts,
        experts,
        experts,
    )
    return jax.shard_map(local, mesh=mesh, in_specs=in_specs, out_specs=out_specs, check_vma=False)
```

```python
import jax
import jax.numpy as jnp
from jax import lax
from jax.sharding import PartitionSpec as P

EPSILON = 1e-06
BF = jnp.bfloat16
F32 = jnp.float32
CAP = 12
EARLY = 8
DW_CUT = 1280
TP = 4

UP = [(i, (i + 1) % TP) for i in range(TP)]
DOWN = [(i, (i - 1) % TP) for i in range(TP)]
MIRROR = [(i, TP - 1 - i) for i in range(TP)]
TWIN = [(i, i ^ 1) for i in range(TP)]


def shift(block, route):
    return lax.ppermute(block, "tp", route)


def dotf(a, b, dims=((1,), (0,))):
    return lax.dot_general(a, b, (dims, ((), ())), preferred_element_type=F32)


def rms_inverse(hidden):
    return lax.rsqrt(jnp.mean(hidden * hidden, axis=-1, keepdims=True) + EPSILON)


def rms_grad(hidden, gain_vec, inv_rms, grad_out):
    normed = hidden * inv_rms
    grad_normed = grad_out * gain_vec
    return inv_rms * (grad_normed - normed * jnp.mean(grad_normed * normed, axis=-1, keepdims=True))


def block_of(rows, offset):
    z = lax.axis_index("tp")
    parts = rows.reshape(TP, rows.shape[0] // TP, rows.shape[1])
    return lax.dynamic_index_in_dim(parts, (z + offset) % TP, 0, keepdims=False)


def ring_order(rows):
    return jnp.concatenate([block_of(rows, j) for j in (2, 1, 3, 0)], 0)


def ring_reduce(ordered, weights):
    half = weights.shape[1] // 2
    size = ordered.shape[0] // TP
    far = dotf(ordered[:size], weights).astype(BF)
    from_below = shift(far[:, :half], UP)
    from_above = shift(far[:, half:], DOWN)
    near = dotf(ordered[size:], weights)
    above, below, own = near[:size], near[size : 2 * size], near[2 * size :]
    to_above = jnp.concatenate([above[:, :half] + from_below.astype(F32), above[:, half:]], 1)
    to_below = jnp.concatenate([below[:, :half], below[:, half:] + from_above.astype(F32)], 1)
    got_up = shift(to_above.astype(BF), UP)
    got_down = shift(to_below.astype(BF), DOWN)
    return own + got_up.astype(F32) + got_down.astype(F32)


def ring_gather(rows):
    half = rows.shape[1] // 2
    below = shift(rows, UP)
    above = shift(rows, DOWN)
    far_left = shift(below[:, :half], UP)
    far_right = shift(above[:, half:], DOWN)
    return rows, above, jnp.concatenate([far_left, far_right], 1), below


def place(blocks):
    z = lax.axis_index("tp")
    out = jnp.zeros((TP,) + blocks[0].shape, blocks[0].dtype)
    for j, block in enumerate(blocks):
        out = lax.dynamic_update_index_in_dim(out, block, (z + j) % TP, 0)
    return out.reshape(TP * blocks[0].shape[0], blocks[0].shape[1])


def exchange(rows):
    count = lax.axis_size("ctx")
    blocks = rows.reshape(count, rows.shape[0] // count, rows.shape[1])
    moved = lax.all_to_all(blocks, "ctx", split_axis=0, concat_axis=0, tiled=True)
    return moved.reshape(rows.shape)


def split_low(values):
    high = values.astype(BF)
    return jnp.concatenate([high, (values - high.astype(F32)).astype(BF)], 1)


def both(pair):
    half = pair.shape[0] // 2
    return pair[:half] + pair[half:]


def expert_forward(rows, w_all, down_all):
    ff = w_all.shape[1] // 4
    pre = dotf(rows, w_all)
    pre_gate = jnp.concatenate([pre[:, :ff], pre[:, 2 * ff : 3 * ff]], 1)
    pre_up = jnp.concatenate([pre[:, ff : 2 * ff], pre[:, 3 * ff :]], 1)
    active = (jax.nn.silu(pre_gate) * pre_up).astype(BF)
    return pre_gate, pre_up, active, dotf(active, down_all).astype(BF)


def expert_backward(grads, pre_gate, pre_up, w_all, down_all):
    ff = w_all.shape[1] // 4
    sigmoid_gate = jax.nn.sigmoid(pre_gate)
    grad_active = dotf(grads, down_all, ((1,), (1,)))
    grad_gate = (
        grad_active * pre_up * sigmoid_gate * (1.0 + pre_gate * (1.0 - sigmoid_gate))
    ).astype(BF)
    grad_up = (grad_active * (pre_gate * sigmoid_gate)).astype(BF)
    grad_all = jnp.concatenate(
        [grad_gate[:, :ff], grad_up[:, :ff], grad_gate[:, ff:], grad_up[:, ff:]], 1
    )
    return grad_all, dotf(grad_all, w_all, ((1,), (1,))).astype(BF)


def local(
    attention,
    residual,
    w_out,
    w_qkv,
    norm_moe,
    norm_attn,
    expert_ids,
    expert_gates,
    w_gate,
    w_up,
    w_down,
    d_projected,
    d_stream,
):
    ctx_count = lax.axis_size("ctx")
    tokens, width = residual.shape
    kind = lax.axis_index("tp") // 2

    gate_mine, up_mine, down_mine = w_gate[0], w_up[0], w_down[0]
    ff = gate_mine.shape[1]
    gate_twin = jnp.concatenate(
        [shift(gate_mine[low:high], TWIN) for low, high in ((0, 256), (256, 1024), (1024, width))],
        0,
    )
    up_twin = shift(up_mine, TWIN)
    down_twin = shift(down_mine, TWIN)

    table = jnp.concatenate([expert_ids.astype(F32), expert_gates], 1).T
    table = jnp.concatenate([table, shift(table, MIRROR)], 1)
    top = expert_ids.shape[1]
    ids_t = table[:top].astype(jnp.int32)
    gates_t = table[top:]
    wanted = 2 * jnp.arange(ctx_count, dtype=jnp.int32) + kind
    same = ids_t[:, None, :] == wanted[None, :, None]
    member = jnp.any(same, axis=0)
    gate_of = jnp.sum(jnp.where(same, gates_t[:, None, :], 0.0), axis=0)
    token = jnp.arange(2 * tokens, dtype=jnp.int32)
    mirrored = token >= tokens
    earlier = (token[:, None] < token[None, :]) & (mirrored[:, None] == mirrored[None, :])
    position = dotf(member.astype(BF), earlier.astype(BF)).astype(jnp.int32)

    late_count = 2 * CAP - EARLY
    early_at = jnp.where(member, position, -1)[:, :tokens]
    late_at = jnp.where(member, position + jnp.where(mirrored, CAP - EARLY, -EARLY)[None, :], -1)
    early_is = early_at[:, None, :] == jnp.arange(EARLY, dtype=jnp.int32)[None, :, None]
    late_is = late_at[:, None, :] == jnp.arange(late_count, dtype=jnp.int32)[None, :, None]
    early = early_is.astype(BF).reshape(ctx_count * EARLY, tokens)
    late = late_is.astype(BF).reshape(ctx_count * late_count, 2 * tokens)
    early_gated = jnp.where(early_is, gate_of[:, None, :tokens], 0.0).reshape(early.shape)
    late_gated = jnp.where(late_is, gate_of[:, None, :], 0.0).reshape(late.shape)
    early_gate = jnp.sum(early_gated, axis=1, keepdims=True)
    late_gate = jnp.sum(late_gated, axis=1, keepdims=True)
    early_own = split_low(early_gated)
    late_own = split_low(late_gated[:, :tokens])
    late_mirror = split_low(late_gated[:, tokens:])

    attn_rel = ring_order(attention)
    hidden = residual.astype(F32) + ring_reduce(attn_rel, w_out)
    inv_one = rms_inverse(hidden)
    moe_input = (hidden * inv_one * norm_moe).astype(BF)
    early_rows = exchange(dotf(early, moe_input).astype(BF))
    inputs = jnp.concatenate([moe_input, shift(moe_input, MIRROR)], 0)
    late_rows = exchange(dotf(late, inputs).astype(BF))

    w_all = jnp.concatenate([gate_mine, up_mine, gate_twin, up_twin], 1)
    down_all = jnp.concatenate([down_mine, down_twin], 0)
    early_pg, early_pu, early_act, early_out = expert_forward(early_rows, w_all, down_all)
    late_pg, late_pu, late_act, late_out = expert_forward(late_rows, w_all, down_all)
    late_ret = exchange(late_out)
    early_ret = exchange(early_out)

    over = ((0,), (0,))
    moe_got = shift(both(dotf(late_mirror, late_ret, over)).astype(BF), MIRROR)
    moe_own = both(dotf(late_own, late_ret, over) + dotf(early_own, early_ret, over))
    stream_sum = hidden + (moe_own + moe_got.astype(F32))
    stream = stream_sum.astype(BF)
    inv_two = rms_inverse(stream_sum)
    attn_input = (stream_sum * inv_two * norm_attn).astype(BF)

    grad_attn_in = ring_reduce(ring_order(d_projected), w_qkv)
    grad_stream = d_stream.astype(F32) + rms_grad(stream_sum, norm_attn, inv_two, grad_attn_in)
    grad_bf = grad_stream.astype(BF)
    early_grads = exchange((dotf(early, grad_bf) * early_gate).astype(BF))
    grad_pair = jnp.concatenate([grad_bf, shift(grad_bf, MIRROR)], 0)
    late_grads = exchange((dotf(late, grad_pair) * late_gate).astype(BF))

    early_da, early_in = expert_backward(early_grads, early_pg, early_pu, w_all, down_all)
    early_dw = tuple(
        dotf(a, b, over)
        for a, b in (
            (early_act[:, ff:], early_grads),
            (early_rows, early_da[:, 2 * ff :]),
            (early_act[:, :ff], early_grads),
            (early_rows, early_da[:, : 2 * ff]),
        )
    )
    early_dw = lax.optimization_barrier(early_dw)
    down_part = (early_dw[0] + dotf(late_act[:, ff:], late_grads, over)).astype(BF)
    down_got = shift(down_part, TWIN)
    late_grads, down_part = lax.optimization_barrier((late_grads, down_part))
    late_da, late_in = expert_backward(late_grads, late_pg, late_pu, w_all, down_all)
    late_back = exchange(late_in)
    early_back = exchange(early_in)
    pair_part = (early_dw[1] + dotf(late_rows, late_da[:, 2 * ff :], over)).astype(BF)
    pair_got = jnp.concatenate(
        [shift(pair_part[:DW_CUT], TWIN), shift(pair_part[DW_CUT:], TWIN)], 0
    )

    back_got = shift(dotf(late[:, tokens:], late_back, over).astype(BF), MIRROR)
    grad_moe_in = dotf(late[:, :tokens], late_back, over) + dotf(early, early_back, over)
    grad_moe_in = grad_moe_in + back_got.astype(F32)
    grad_hidden = grad_stream + rms_grad(hidden, norm_moe, inv_one, grad_moe_in)
    grad_residual = grad_hidden.astype(BF)

    grad_blocks = ring_gather(grad_residual)
    grad_rows = jnp.concatenate([grad_blocks[j] for j in (2, 1, 3, 0)], 0)
    out_partial = dotf(grad_rows, attn_rel, over).astype(BF)
    cores = out_partial.reshape(ctx_count // 2, 2, 2 * width // (2 * ctx_count), -1)
    core = lax.axis_index("ctx") % 2
    given = lax.dynamic_index_in_dim(cores, 1 - core, 1, keepdims=False)
    kept = lax.dynamic_index_in_dim(cores, core, 1, keepdims=False)
    got = lax.ppermute(given, "ctx", [(i, i ^ 1) for i in range(ctx_count)])
    chip_part = (kept.astype(F32) + got.astype(F32)).astype(BF)
    same_core = [list(range(i, ctx_count, 2)) for i in range(2)]
    out_moved = lax.all_to_all(
        chip_part, "ctx", split_axis=0, concat_axis=0, axis_index_groups=same_core, tiled=True
    )
    out_weight_grad = jnp.sum(out_moved.astype(F32), axis=0).T.astype(BF)
    grad_attention = place([dotf(g, w_out, ((1,), (1,))).astype(BF) for g in grad_blocks])
    attn_blocks = ring_gather(attn_input)
    projected = place([dotf(a, w_qkv, ((1,), (1,))).astype(BF) for a in attn_blocks])

    down_grad = early_dw[2] + dotf(late_act[:, :ff], late_grads, over)
    down_grad = (down_grad + down_got.astype(F32)).astype(BF)
    pair_grad = early_dw[3] + dotf(late_rows, late_da[:, : 2 * ff], over)
    pair_grad = (pair_grad + pair_got.astype(F32)).astype(BF)
    return (
        projected,
        stream,
        grad_attention,
        grad_residual,
        out_weight_grad,
        pair_grad[:, :ff][None],
        pair_grad[:, ff:][None],
        down_grad[None],
    )


def solution(mesh):
    token_rows = P(("ctx", "tp"), None)
    experts = P(("ctx", "tp"), None, None)
    in_specs = (
        P("ctx", "tp"),
        token_rows,
        P("tp", None),
        P("tp", None),
        P(),
        P(),
        token_rows,
        token_rows,
        experts,
        experts,
        experts,
        P("ctx", "tp"),
        token_rows,
    )
    out_specs = (
        P("ctx", "tp"),
        token_rows,
        P("ctx", "tp"),
        token_rows,
        P("tp", "ctx"),
        experts,
        experts,
        experts,
    )
    return jax.shard_map(local, mesh=mesh, in_specs=in_specs, out_specs=out_specs, check_vma=False)
```
